256 devices in a mesh: dp: 32 (over x, z), expert: 8 (over y, core).
Axes of the slice: x: 4, y: 4, z: 8, core: 2. Of those that a mesh axis runs over, the one named last changes fastest.
Arguments:
- x_act: bfloat16 [32, 4, 256, 4096], P('dp', None, None, 'expert'), may hold values from -16 to 16
- d_out: bfloat16 [32, 4, 256, 1536], P('dp'), may hold values from -0.375 to 0.375
- error: bfloat16 [32, 4, 4096, 1536], P('dp', None, 'expert'), may hold values from -6 to 6
- q_init: bfloat16 [1536, 256], replicated, may hold values from -6 to 6
- modality: int32 [4], replicated, may hold values from 0 to 1, as said below
- membership: int32 [32], replicated, may hold values from 0 to 3, as said below
Outputs:
- q_sum: bfloat16 [32, 1536, 256], P('dp')
- error_new: bfloat16 [32, 4, 4096, 1536], P('dp', None, 'expert')
The draws below stay inside these ranges and needn't reach their ends.
Inputs may be any that keep to these rules, and one draw needn't show every extreme that they name: Half of the experts have modality 0 and half modality 1. `membership`: each text replica group holds exactly 8 data replicas.
All inputs are finite; a program needn't handle non-finite values.
Results may differ from the reference program's by a relative error of at most 0.005.
Values may be sent and summed in bfloat16 or wider, within the bound.
No kernel may reach another device: no remote copies, remote signals or barrier semaphores. Data moves between devices by JAX's collectives and lax.ppermute only.
A program may use at most 128 MiB of HBM per device.

```python
import jax
import jax.numpy as jnp
from jax import lax

D = 4096
H = 1536
R = 64
GROUPS = 4
EXPERTS = 4
TOK = 256
REPL = 8
N_DP = 32


def draw_modality(key, part):
    return (jax.random.permutation(key, EXPERTS) % 2).astype(jnp.int32)


def draw_membership(key, part):
    return (jax.random.permutation(key, GROUPS * REPL) // REPL).astype(jnp.int32)


def draw_x_act(key, part):
    key_rough, key_noise = jax.random.split(jax.random.fold_in(key, 17), 2)
    replicas = GROUPS * REPL
    feature = jnp.arange(D, dtype=jnp.float32) / D
    tilt = jnp.exp(jnp.log(3.0) * (feature - 0.5))
    rough = jnp.exp(jax.random.uniform(key_rough, (replicas, EXPERTS, 1, D), minval=-1.15, maxval=1.15))
    noise = jnp.clip(jax.random.normal(key_noise, (replicas, EXPERTS, TOK, D)), -4.0, 4.0)
    return jnp.clip(noise * rough * tilt, -16.0, 16.0).astype(jnp.bfloat16)


def steps_of(rng, shape, cuts, least, high):
    loudness, own = 1.0, jax.random.fold_in(rng, 6)
    for axis_at, parts in cuts:
        draws = jnp.exp(jax.random.uniform(jax.random.fold_in(own, axis_at), (parts,), jnp.float32, least / len(cuts), high / len(cuts)))
        loudness = loudness * jnp.repeat(draws, shape[axis_at] // parts).reshape([-1 if axis == axis_at else 1 for axis in range(len(shape))])
    return loudness


def gaussian(stream_key, extent, spread, most, shards=(), held_as=jnp.bfloat16):
    level = steps_of(stream_key, extent, shards, -0.22, 0.18) if shards else 1.0
    entries = jax.random.normal(stream_key, extent, jnp.float32) * spread * level
    return jnp.minimum(jnp.maximum(entries, -most), most).astype(held_as)


def setup_inputs(seed: int = 0) -> dict:
    splits = jax.random.split(jax.random.key(seed), 7)
    x_act = draw_x_act(jax.random.fold_in(splits[6], 71), 0)
    d_out = gaussian(splits[1], (N_DP, EXPERTS, TOK, H), (TOK ** -0.5), 0.375, ((0, 32),))
    error = gaussian(splits[2], (N_DP, EXPERTS, D, H), 1.0, 6.0, ((0, 32), (2, 8)))
    q_init = gaussian(splits[3], (H, EXPERTS * R), 1.0, 6.0)
    modality = draw_modality(jax.random.fold_in(splits[6], 71), 0)
    membership = draw_membership(jax.random.fold_in(splits[6], 71), 0)
    return {"x_act": x_act, "d_out": d_out, "error": error, "q_init": q_init, "modality": modality, "membership": membership}


highest = lax.Precision.HIGHEST

def average(values, modality, membership):
    replicas = membership.shape[0]
    same_group = (membership[:, None] == membership[None, :]).astype(jnp.float32) / REPL
    group_mean = jnp.einsum('ij,jabc->iabc', same_group, values, precision=highest)
    whole_mean = jnp.broadcast_to(jnp.sum(values, axis=0, keepdims=True) / replicas, values.shape)
    image_blocks = (modality == 0)[:, None]
    return jnp.where(image_blocks, whole_mean, group_mean)

def reference(x_act, d_out, error, q_init, modality, membership):
    q_blocks = q_init.reshape(H, EXPERTS, R).astype(jnp.float32)

    def left_of(inputs):
        tok_x, grads_out, residual = inputs
        gradient = jnp.einsum('ktd,kth->kdh', tok_x.astype(jnp.float32), grads_out.astype(jnp.float32), precision=highest)
        merged = (gradient + residual.astype(jnp.float32)).astype(jnp.bfloat16)
        left_part = jnp.einsum('kdh,hkr->dkr', merged.astype(jnp.float32), q_blocks, precision=highest)
        return (merged, left_part)
    merged, left_part = lax.map(left_of, (x_act, d_out, error))
    left_mean = average(left_part, modality, membership)
    gram_block = jnp.einsum('idkr,idks->ikrs', left_mean, left_mean, precision=highest)
    identity = jnp.eye(R, dtype=jnp.float32)
    shift_term = 0.001 * jnp.trace(gram_block, axis1=2, axis2=3) / R
    factor_low = jnp.linalg.cholesky(gram_block + shift_term[:, :, None, None] * identity)
    inverse = jax.scipy.linalg.solve_triangular(factor_low, jnp.broadcast_to(identity, factor_low.shape), lower=True)
    p_hat = jnp.einsum('idkr,iksr->idks', left_mean, inverse, precision=highest).astype(jnp.bfloat16)

    def right_of(inputs):
        merged_one, p_one = inputs
        return jnp.einsum('kdh,dkr->hkr', merged_one.astype(jnp.float32), p_one.astype(jnp.float32), precision=highest)
    q_local = lax.map(right_of, (merged, p_hat))
    q_sum = average(q_local, modality, membership).astype(jnp.bfloat16)

    def error_of(inputs):
        merged_one, p_one, q_one = inputs
        approx = jnp.einsum('dkr,hkr->kdh', p_one.astype(jnp.float32), q_one.astype(jnp.float32), precision=highest)
        return (merged_one.astype(jnp.float32) - approx).astype(jnp.bfloat16)
    error_new = lax.map(error_of, (merged, p_hat, q_sum))
    replicas = membership.shape[0]
    return (q_sum.reshape(replicas, H, EXPERTS * R), error_new)
```

```python
import functools

import jax
import jax.numpy as jnp
from jax import lax
from jax.experimental import pallas as pl
from jax.experimental.pallas import tpu as pltpu
from jax.sharding import PartitionSpec as P

GROUPS = 4
F32 = jnp.float32
BF16 = jnp.bfloat16
HIGHEST = lax.Precision.HIGHEST
SMEM = pltpu.SMEM
VMEM = pltpu.VMEM


def dot(a, b, ca, cb, precision=None):
    return lax.dot_general(
        a, b, (((ca,), (cb,)), ((), ())), precision=precision, preferred_element_type=F32
    )


def params(mib=40, **kw):
    return pltpu.CompilerParams(vmem_limit_bytes=mib << 20, **kw)


def merge_kernel(x_ref, d_ref, e_ref, q_ref, merged_ref, left_ref):
    k = pl.program_id(0)
    rank = q_ref.shape[1] // pl.num_programs(0)
    xt = x_ref[0, 0].T
    rows = xt.shape[0]
    hidden = d_ref.shape[3]
    step = 256
    acc = jnp.zeros((rows, q_ref.shape[1]), F32)
    for n in range(0, hidden, step):
        cols = pl.ds(n, step)
        grad = dot(xt, d_ref[0, 0, :, cols], 1, 0)
        m = (grad + e_ref[0, 0, :, cols].astype(F32)).astype(BF16)
        merged_ref[0, :, cols] = m
        acc = acc + dot(m, q_ref[cols, :], 1, 0)
    acc = acc.reshape(left_ref.shape)
    owner = lax.broadcasted_iota(jnp.int32, acc.shape, 2) // rank
    left_ref[...] = jnp.where(owner == k, acc, left_ref[...])


def merge(x_act, d_out, error, q_init, parts):
    _, experts, tok, rows = x_act.shape
    hidden = d_out.shape[3]
    width = q_init.shape[1]
    return pl.pallas_call(
        merge_kernel,
        grid=(experts,),
        in_specs=[
            pl.BlockSpec((1, 1, tok, rows), lambda k: (0, k, 0, 0)),
            pl.BlockSpec((1, 1, tok, hidden), lambda k: (0, k, 0, 0)),
            pl.BlockSpec((1, 1, rows, hidden), lambda k: (0, k, 0, 0)),
            pl.BlockSpec((hidden, width), lambda k: (0, 0)),
        ],
        out_specs=[
            pl.BlockSpec((1, rows, hidden), lambda k: (k, 0, 0)),
            pl.BlockSpec((parts, rows // parts, width), lambda k: (0, 0, 0)),
        ],
        out_shape=[
            jax.ShapeDtypeStruct((experts, rows, hidden), BF16),
            jax.ShapeDtypeStruct((parts, rows // parts, width), F32),
        ],
        compiler_params=params(),
        name="merge",
    )(x_act, d_out, error, q_init)


def group_sums(member_ref, x_ref):
    replicas = x_ref.shape[0]
    sums = [jnp.zeros(x_ref.shape[1:], F32) for _ in range(GROUPS)]
    for j in range(replicas):
        v = x_ref[j]
        for g in range(GROUPS):
            sums[g] = sums[g] + jnp.where(member_ref[j] == g, v, 0.0)
    return sums


def mean_left_kernel(member_ref, mod_ref, x_ref, o_ref, g_ref):
    replicas, rows, width = x_ref.shape
    experts = mod_ref.shape[0]
    rank = width // experts
    sums = group_sums(member_ref, x_ref)
    whole = sums[0] + sums[1] + sums[2] + sums[3]
    owner = lax.broadcasted_iota(jnp.int32, (rows, width), 1) // rank
    image = jnp.zeros((rows, width), jnp.int32)
    for k in range(experts):
        flag = (mod_ref[k] == 0).astype(jnp.int32)
        image = jnp.where(owner == k, flag, image)
    for g in range(GROUPS):
        g_ref[g] = jnp.where(
            image == 1, whole * (1.0 / replicas), sums[g] * (GROUPS / replicas)
        )
    for j in range(replicas):
        o_ref[j] = g_ref[member_ref[j]]


def mean_left(membership, modality, x):
    return pl.pallas_call(
        mean_left_kernel,
        in_specs=[
            pl.BlockSpec(memory_space=SMEM),
            pl.BlockSpec(memory_space=SMEM),
            pl.BlockSpec(memory_space=VMEM),
        ],
        out_specs=pl.BlockSpec(memory_space=VMEM),
        out_shape=jax.ShapeDtypeStruct(x.shape, F32),
        scratch_shapes=[VMEM((GROUPS,) + x.shape[1:], F32)],
        compiler_params=params(16),
        name="mean_left",
    )(membership, modality, x)


def mean_right_kernel(rank, member_ref, mod_ref, place_ref, x_ref, o_ref, g_ref):
    replicas = x_ref.shape[0]
    column = place_ref[1] * replicas + place_ref[0]
    image = mod_ref[column // rank] == 0
    sums = group_sums(member_ref, x_ref)
    whole = sums[0] + sums[1] + sums[2] + sums[3]
    for g in range(GROUPS):
        g_ref[g] = jnp.where(image, whole * (1.0 / replicas), sums[g] * (GROUPS / replicas))
    for j in range(replicas):
        o_ref[j] = g_ref[member_ref[j]]


def mean_right(membership, modality, place, x, rank):
    return pl.pallas_call(
        functools.partial(mean_right_kernel, rank),
        in_specs=[pl.BlockSpec(memory_space=SMEM)] * 3 + [pl.BlockSpec(memory_space=VMEM)],
        out_specs=pl.BlockSpec(memory_space=VMEM),
        out_shape=jax.ShapeDtypeStruct(x.shape, F32),
        scratch_shapes=[VMEM((GROUPS,) + x.shape[1:], F32)],
        compiler_params=params(16),
        name="mean_right",
    )(membership, modality, place, x)


def gram_kernel(rank, x_ref, o_ref):
    x = x_ref[...].reshape(-1, x_ref.shape[2])
    full = dot(x.T, x, 1, 0, HIGHEST)
    for k in range(x.shape[1] // rank):
        block = slice(k * rank, (k + 1) * rank)
        o_ref[:, block] = full[block, block]


def gram(left_mean, rank):
    return pl.pallas_call(
        functools.partial(gram_kernel, rank),
        in_specs=[pl.BlockSpec(memory_space=VMEM)],
        out_specs=pl.BlockSpec(memory_space=VMEM),
        out_shape=jax.ShapeDtypeStruct((rank, left_mean.shape[2]), F32),
        compiler_params=params(16),
        name="gram",
    )(left_mean)


def inverse_factors(grams, inv_ref, rank):
    width = 2 * rank
    experts = grams.shape[1] // rank
    row = lax.broadcasted_iota(jnp.int32, (rank, width), 0)
    lane = lax.broadcasted_iota(jnp.int32, (rank, width), 1)
    eye = (row == lax.rem(lane, rank)).astype(F32)
    inv_ref[...] = jnp.zeros_like(inv_ref)
    systems = []
    for k in range(experts):
        pair = grams[:, (k // 2) * width : (k // 2 + 1) * width]
        turned = pltpu.roll(pair, rank, 1)
        mine = (lane >= rank) if k % 2 == 0 else (lane < rank)
        trace = jnp.sum(jnp.where(mine, turned * eye, 0.0), keepdims=True)
        shifted = turned + eye * (0.001 * trace / rank)
        systems.append(jnp.where(mine, shifted, eye))
    for j in range(rank):
        for k in range(experts):
            at = j + (rank if k % 2 == 0 else 0)
            m = systems[k]
            pivot_row = m[j : j + 1, :]
            pivot = pivot_row[:, at : at + 1]
            other = (lane[:1] < rank) if k % 2 == 0 else (lane[:1] >= rank)
            inv_ref[k * rank + j : k * rank + j + 1, (k // 2) * width : (k // 2 + 1) * width] = (
                jnp.where(other, pivot_row * lax.rsqrt(pivot), 0.0)
            )
            if j + 1 < rank:
                scaled = pivot_row * (1.0 / pivot)
                factor = jnp.where(row[:, :1] > j, m[:, at : at + 1], 0.0)
                systems[k] = m - factor * scaled


def right_kernel(
    rank, g0, g1, g2, g3, g4, g5, g6, g7, left_ref, merged_ref, pt_ref, qt_ref, inv_ref, psc_ref
):
    k = pl.program_id(0)

    @pl.when(k == 0)
    def _():
        grams = ((g0[...] + g1[...]) + (g2[...] + g3[...])) + (
            (g4[...] + g5[...]) + (g6[...] + g7[...])
        )
        inverse_factors(grams, inv_ref, rank)
        left = left_ref[...].reshape(-1, left_ref.shape[2])
        pt = dot(inv_ref[...], left, 1, 1, HIGHEST).astype(BF16)
        psc_ref[...] = pt
        pt_ref[...] = pt

    rows = pl.ds(pl.multiple_of(k * rank, rank), rank)
    q = dot(psc_ref[rows, :], merged_ref[0], 1, 0).astype(BF16)
    qt_ref[...] = q.reshape(qt_ref.shape)


def right(grams, left_mean, merged, shares):
    experts, rows, hidden = merged.shape
    width = left_mean.shape[2]
    rank = width // experts
    whole = pl.BlockSpec((rank, width), lambda k: (0, 0))
    return pl.pallas_call(
        functools.partial(right_kernel, rank),
        grid=(experts,),
        in_specs=[whole] * 8
        + [
            pl.BlockSpec(left_mean.shape, lambda k: (0, 0, 0)),
            pl.BlockSpec((1, rows, hidden), lambda k: (k, 0, 0)),
        ],
        out_specs=[
            pl.BlockSpec((width, rows), lambda k: (0, 0)),
            pl.BlockSpec((shares // experts, width // shares, hidden), lambda k: (k, 0, 0)),
        ],
        out_shape=[
            jax.ShapeDtypeStruct((width, rows), BF16),
            jax.ShapeDtypeStruct((shares, width // shares, hidden), BF16),
        ],
        scratch_shapes=[VMEM((width, width), F32), VMEM((width, rows), BF16)],
        compiler_params=params(),
        name="right",
    )(*grams, left_mean, merged)


def share_sum_kernel(x_ref, o_ref):
    total = x_ref[0].astype(F32)
    for e in range(1, x_ref.shape[0]):
        total = total + x_ref[e].astype(F32)
    for c in range(o_ref.shape[1]):
        o_ref[:, c, :] = total[:, c * 128 : (c + 1) * 128]


def share_sum(x):
    _, columns, hidden = x.shape
    return pl.pallas_call(
        share_sum_kernel,
        in_specs=[pl.BlockSpec(memory_space=VMEM)],
        out_specs=pl.BlockSpec(memory_space=VMEM),
        out_shape=jax.ShapeDtypeStruct((columns, hidden // 128, 128), F32),
        compiler_params=params(16),
        name="share_sum",
    )(x)


def pack_kernel(x_ref, o_ref):
    for s in range(o_ref.shape[0]):
        for c in range(x_ref.shape[1]):
            o_ref[s, :, c * 128 : (c + 1) * 128] = x_ref[:, c, :].astype(BF16)


def pack(x, shares):
    columns, tiles, lanes = x.shape
    return pl.pallas_call(
        pack_kernel,
        in_specs=[pl.BlockSpec(memory_space=VMEM)],
        out_specs=pl.BlockSpec(memory_space=VMEM),
        out_shape=jax.ShapeDtypeStruct((shares, columns, tiles * lanes), BF16),
        compiler_params=params(16),
        name="pack",
    )(x)


def error_kernel(rank, pt_ref, qt_ref, merged_ref, q_ref, e_ref):
    k = pl.program_id(0)

    @pl.when(k == 0)
    def _():
        q_ref[0] = qt_ref[...].T

    rows = pl.ds(pl.multiple_of(k * rank, rank), rank)
    p = pt_ref[rows, :].T
    hidden = merged_ref.shape[2]
    for n in range(0, hidden, 256):
        cols = pl.ds(n, 256)
        approx = dot(p, qt_ref[rows, cols], 1, 0)
        e_ref[0, 0, :, cols] = (merged_ref[0, :, cols].astype(F32) - approx).astype(BF16)


def error_of(pt, qt, merged):
    experts, rows, hidden = merged.shape
    width = pt.shape[0]
    return pl.pallas_call(
        functools.partial(error_kernel, width // experts),
        grid=(experts,),
        in_specs=[
            pl.BlockSpec((width, rows), lambda k: (0, 0)),
            pl.BlockSpec((width, hidden), lambda k: (0, 0)),
            pl.BlockSpec((1, rows, hidden), lambda k: (k, 0, 0)),
        ],
        out_specs=[
            pl.BlockSpec((1, hidden, width), lambda k: (0, 0, 0)),
            pl.BlockSpec((1, 1, rows, hidden), lambda k: (0, k, 0, 0)),
        ],
        out_shape=[
            jax.ShapeDtypeStruct((1, hidden, width), BF16),
            jax.ShapeDtypeStruct((1, experts, rows, hidden), BF16),
        ],
        compiler_params=params(),
        name="error_of",
    )(pt, qt, merged)


def exchange(x, axis):
    return lax.all_to_all(x, axis, 0, 0, tiled=True)


def on_device(x_act, d_out, error, q_init, modality, membership):
    experts = x_act.shape[1]
    width = q_init.shape[1]
    rank = width // experts
    replicas = membership.shape[0]
    shares = lax.axis_size("expert")
    place = jnp.stack([lax.axis_index("dp"), lax.axis_index("expert")]).astype(jnp.int32)

    merged, left = merge(x_act, d_out, error, q_init, replicas)
    chunks = exchange(left, "dp")
    left_mean = exchange(mean_left(membership, modality, chunks), "dp")
    part = gram(left_mean, rank)
    grams = [part] + [
        lax.ppermute(part, "expert", [(i, i ^ s) for i in range(shares)])
        for s in range(1, shares)
    ]
    pt, qt = right(grams, left_mean, merged, shares)
    columns = share_sum(exchange(qt, "expert"))
    means = mean_right(membership, modality, place, exchange(columns, "dp"), rank)
    mine = pack(exchange(means, "dp"), shares)
    q_rows = exchange(mine, "expert").reshape(width, -1)
    return tuple(error_of(pt, q_rows, merged))


def solution(mesh):
    in_specs = (
        P("dp", None, None, "expert"),
        P("dp", None, None, None),
        P("dp", None, "expert", None),
        P(),
        P(),
        P(),
    )
    out_specs = (P("dp", None, None), P("dp", None, "expert", None))
    return jax.shard_map(
        on_device, mesh=mesh, in_specs=in_specs, out_specs=out_specs, check_vma=False
    )
```

```python
import functools

import jax
import jax.numpy as jnp
from jax import lax
from jax.experimental import pallas as pl
from jax.experimental.pallas import tpu as pltpu
from jax.sharding import PartitionSpec as P

GROUPS = 4
F32 = jnp.float32
BF16 = jnp.bfloat16
HIGHEST = lax.Precision.HIGHEST
SMEM = pltpu.SMEM
VMEM = pltpu.VMEM
BIG = 26


def dot(a, b, ca, cb, precision=None):
    return lax.dot_general(
        a, b, (((ca,), (cb,)), ((), ())), precision=precision, preferred_element_type=F32
    )


def params(mib=40, **kw):
    return pltpu.CompilerParams(vmem_limit_bytes=mib << 20, **kw)


def merge_kernel(x_ref, d_ref, e_ref, q_ref, merged_ref, left_ref):
    k = pl.program_id(0)
    rank = q_ref.shape[1] // pl.num_programs(0)
    xt = x_ref[0, 0].T
    rows = xt.shape[0]
    hidden = d_ref.shape[3]
    step = 256
    acc = jnp.zeros((rows, q_ref.shape[1]), F32)
    for n in range(0, hidden, step):
        cols = pl.ds(n, step)
        grad = dot(xt, d_ref[0, 0, :, cols], 1, 0)
        m = (grad + e_ref[0, 0, :, cols].astype(F32)).astype(BF16)
        merged_ref[0, :, cols] = m
        acc = acc + dot(m, q_ref[cols, :], 1, 0)
    acc = acc.reshape(left_ref.shape)
    owner = lax.broadcasted_iota(jnp.int32, acc.shape, 2) // rank
    left_ref[...] = jnp.where(owner == k, acc, left_ref[...])


def merge(x_act, d_out, error, q_init, parts):
    _, experts, tok, rows = x_act.shape
    hidden = d_out.shape[3]
    width = q_init.shape[1]
    return pl.pallas_call(
        merge_kernel,
        grid=(experts,),
        in_specs=[
            pl.BlockSpec((1, 1, tok, rows), lambda k: (0, k, 0, 0)),
            pl.BlockSpec((1, 1, tok, hidden), lambda k: (0, k, 0, 0)),
            pl.BlockSpec((1, 1, rows, hidden), lambda k: (0, k, 0, 0)),
            pl.BlockSpec((hidden, width), lambda k: (0, 0)),
        ],
        out_specs=[
            pl.BlockSpec((1, rows, hidden), lambda k: (k, 0, 0)),
            pl.BlockSpec((parts, rows // parts, width), lambda k: (0, 0, 0)),
        ],
        out_shape=[
            jax.ShapeDtypeStruct((experts, rows, hidden), BF16),
            jax.ShapeDtypeStruct((parts, rows // parts, width), F32),
        ],
        compiler_params=params(BIG),
        name="merge",
    )(x_act, d_out, error, q_init)


def group_sums(member_ref, x_ref):
    replicas = x_ref.shape[0]
    sums = [jnp.zeros(x_ref.shape[1:], F32) for _ in range(GROUPS)]
    for j in range(replicas):
        v = x_ref[j]
        for g in range(GROUPS):
            sums[g] = sums[g] + jnp.where(member_ref[j] == g, v, 0.0)
    return sums


def mean_left_kernel(member_ref, mod_ref, x_ref, o_ref, g_ref):
    replicas, rows, width = x_ref.shape
    experts = mod_ref.shape[0]
    rank = width // experts
    sums = group_sums(member_ref, x_ref)
    whole = sums[0] + sums[1] + sums[2] + sums[3]
    owner = lax.broadcasted_iota(jnp.int32, (rows, width), 1) // rank
    image = jnp.zeros((rows, width), jnp.int32)
    for k in range(experts):
        flag = (mod_ref[k] == 0).astype(jnp.int32)
        image = jnp.where(owner == k, flag, image)
    for g in range(GROUPS):
        g_ref[g] = jnp.where(
            image == 1, whole * (1.0 / replicas), sums[g] * (GROUPS / replicas)
        )
    for j in range(replicas):
        o_ref[j] = g_ref[member_ref[j]]


def mean_left(membership, modality, x):
    return pl.pallas_call(
        mean_left_kernel,
        in_specs=[
            pl.BlockSpec(memory_space=SMEM),
            pl.BlockSpec(memory_space=SMEM),
            pl.BlockSpec(memory_space=VMEM),
        ],
        out_specs=pl.BlockSpec(memory_space=VMEM),
        out_shape=jax.ShapeDtypeStruct(x.shape, F32),
        scratch_shapes=[VMEM((GROUPS,) + x.shape[1:], F32)],
        compiler_params=params(8),
        name="mean_left",
    )(membership, modality, x)


def mean_right_kernel(member_ref, mod_ref, share_ref, x_ref, o_ref, g_ref):
    replicas = x_ref.shape[0]
    image = mod_ref[share_ref[0] // 2] == 0
    sums = group_sums(member_ref, x_ref)
    whole = sums[0] + sums[1] + sums[2] + sums[3]
    for g in range(GROUPS):
        g_ref[g] = jnp.where(image, whole * (1.0 / replicas), sums[g] * (GROUPS / replicas))
    for j in range(replicas):
        o_ref[j] = g_ref[member_ref[j]]


def mean_right(membership, modality, share, x):
    return pl.pallas_call(
        mean_right_kernel,
        in_specs=[pl.BlockSpec(memory_space=SMEM)] * 3 + [pl.BlockSpec(memory_space=VMEM)],
        out_specs=pl.BlockSpec(memory_space=VMEM),
        out_shape=jax.ShapeDtypeStruct(x.shape, F32),
        scratch_shapes=[VMEM((GROUPS,) + x.shape[1:], F32)],
        compiler_params=params(8),
        name="mean_right",
    )(membership, modality, share, x)


def gram_kernel(rank, x_ref, o_ref):
    x = x_ref[...].reshape(-1, x_ref.shape[2])
    full = dot(x.T, x, 1, 0, HIGHEST)
    for k in range(x.shape[1] // rank):
        block = slice(k * rank, (k + 1) * rank)
        o_ref[:, block] = full[block, block]


def gram(left_mean, rank):
    return pl.pallas_call(
        functools.partial(gram_kernel, rank),
        in_specs=[pl.BlockSpec(memory_space=VMEM)],
        out_specs=pl.BlockSpec(memory_space=VMEM),
        out_shape=jax.ShapeDtypeStruct((rank, left_mean.shape[2]), F32),
        compiler_params=params(8),
        name="gram",
    )(left_mean)


def inverse_factors(grams, inv_ref, rank):
    width = 2 * rank
    experts = grams.shape[1] // rank
    row = lax.broadcasted_iota(jnp.int32, (rank, width), 0)
    lane = lax.broadcasted_iota(jnp.int32, (rank, width), 1)
    eye = (row == lax.rem(lane, rank)).astype(F32)
    inv_ref[...] = jnp.zeros_like(inv_ref)
    systems = []
    for k in range(experts):
        pair = grams[:, (k // 2) * width : (k // 2 + 1) * width]
        turned = pltpu.roll(pair, rank, 1)
        mine = (lane >= rank) if k % 2 == 0 else (lane < rank)
        trace = jnp.sum(jnp.where(mine, turned * eye, 0.0), keepdims=True)
        shifted = turned + eye * (0.001 * trace / rank)
        systems.append(jnp.where(mine, shifted, eye))
    for j in range(rank):
        for k in range(experts):
            at = j + (rank if k % 2 == 0 else 0)
            m = systems[k]
            pivot_row = m[j : j + 1, :]
            pivot = pivot_row[:, at : at + 1]
            other = (lane[:1] < rank) if k % 2 == 0 else (lane[:1] >= rank)
            inv_ref[k * rank + j : k * rank + j + 1, (k // 2) * width : (k // 2 + 1) * width] = (
                jnp.where(other, pivot_row * lax.rsqrt(pivot), 0.0)
            )
            if j + 1 < rank:
                scaled = pivot_row * (1.0 / pivot)
                factor = jnp.where(row[:, :1] > j, m[:, at : at + 1], 0.0)
                systems[k] = m - factor * scaled


def raw_kernel(share_ref, left_ref, merged_ref, keep_ref, send_ref, lt_ref):
    k = pl.program_id(0)
    width = left_ref.shape[2]
    rank = width // pl.num_programs(0)
    half = keep_ref.shape[2]

    @pl.when(k == 0)
    def _():
        lt = left_ref[...].reshape(-1, width).T
        high = lt.astype(BF16)
        low = (lt - high.astype(F32)).astype(BF16)
        for b in range(width // rank):
            rows = slice(b * rank, (b + 1) * rank)
            lt_ref[b, :rank] = high[rows]
            lt_ref[b, rank:] = low[rows]

    both = lt_ref[k]
    core = lax.rem(share_ref[0], 2)
    for h in range(2):
        q = dot(both, merged_ref[0, :, h * half : (h + 1) * half], 1, 0)
        q = q[:rank] + q[rank:]

        @pl.when(core == h)
        def _():
            keep_ref[0] = q

        @pl.when(core != h)
        def _():
            send_ref[0] = q


def raw_right(share, left_mean, merged):
    experts, rows, hidden = merged.shape
    width = left_mean.shape[2]
    rank = width // experts
    half = jax.ShapeDtypeStruct((experts, rank, hidden // 2), F32)
    half_spec = pl.BlockSpec((1, rank, hidden // 2), lambda k, share: (k ^ (share[0] // 2), 0, 0))
    return pl.pallas_call(
        raw_kernel,
        grid_spec=pltpu.PrefetchScalarGridSpec(
            num_scalar_prefetch=1,
            grid=(experts,),
            in_specs=[
                pl.BlockSpec(left_mean.shape, lambda k, share: (0, 0, 0)),
                pl.BlockSpec((1, rows, hidden), lambda k, share: (k, 0, 0)),
            ],
            out_specs=[half_spec, half_spec],
            scratch_shapes=[VMEM((experts, 2 * rank, rows), BF16)],
        ),
        out_shape=[half, half],
        compiler_params=params(BIG),
        name="raw_right",
    )(share, left_mean, merged)


def pair_sum_kernel(a_ref, b_ref, *o_refs):
    for s, o_ref in enumerate(o_refs):
        o_ref[...] = a_ref[s] + b_ref[s]


def pair_sum(a, b):
    piece = jax.ShapeDtypeStruct(a.shape[1:], F32)
    return pl.pallas_call(
        pair_sum_kernel,
        in_specs=[pl.BlockSpec(memory_space=VMEM)] * 2,
        out_specs=[pl.BlockSpec(memory_space=VMEM)] * a.shape[0],
        out_shape=[piece] * a.shape[0],
        compiler_params=params(8),
        name="pair_sum",
    )(a, b)


def share_sum_kernel(a_ref, b_ref, c_ref, d_ref, o_ref):
    total = (a_ref[...] + b_ref[...]) + (c_ref[...] + d_ref[...])
    replicas, tiles, lanes = o_ref.shape
    across = total.shape[1] // lanes
    for t in range(tiles):
        r, c = divmod(t, across)
        o_ref[:, t, :] = total[r * replicas : (r + 1) * replicas, c * lanes : (c + 1) * lanes]


def share_sum(pieces, replicas):
    rank, half = pieces[0].shape
    return pl.pallas_call(
        share_sum_kernel,
        in_specs=[pl.BlockSpec(memory_space=VMEM)] * 4,
        out_specs=pl.BlockSpec(memory_space=VMEM),
        out_shape=jax.ShapeDtypeStruct((replicas, rank * half // (128 * replicas), 128), F32),
        compiler_params=params(8),
        name="share_sum",
    )(*pieces)


def factor_kernel(g0, g1, g2, g3, left_ref, pt_ref, inverse_ref, inv_ref):
    experts, rank, _ = inverse_ref.shape
    inverse_factors((g0[...] + g1[...]) + (g2[...] + g3[...]), inv_ref, rank)
    left = left_ref[...].reshape(-1, left_ref.shape[2])
    pt_ref[...] = dot(inv_ref[...], left, 1, 1, HIGHEST).astype(BF16)
    for k in range(experts):
        block = slice(k * rank, (k + 1) * rank)
        inverse_ref[k] = inv_ref[block, block]


def factor(grams, left_mean):
    rank, width = grams[0].shape
    replicas, rows, _ = left_mean.shape
    return pl.pallas_call(
        factor_kernel,
        in_specs=[pl.BlockSpec(memory_space=VMEM)] * 5,
        out_specs=[pl.BlockSpec(memory_space=VMEM)] * 2,
        out_shape=[
            jax.ShapeDtypeStruct((width, replicas * rows), BF16),
            jax.ShapeDtypeStruct((width // rank, rank, rank), F32),
        ],
        scratch_shapes=[VMEM((width, width), F32)],
        compiler_params=params(8),
        cost_estimate=pl.CostEstimate(flops=1 << 30, bytes_accessed=1 << 20, transcendentals=0),
        name="factor",
    )(*grams, left_mean)


def finish_kernel(share_ref, inverse_ref, x_ref, o_ref, raw_ref):
    replicas, tiles, lanes = x_ref.shape
    across = raw_ref.shape[1] // lanes
    for t in range(tiles):
        r, c = divmod(t, across)
        raw_ref[r * replicas : (r + 1) * replicas, c * lanes : (c + 1) * lanes] = x_ref[:, t, :]
    inverse = inverse_ref[share_ref[0] // 2]
    o_ref[...] = dot(inverse, raw_ref[...], 1, 0, HIGHEST).astype(BF16)


def finish(share, inverse, x):
    rank = inverse.shape[1]
    half = x.size // rank
    return pl.pallas_call(
        finish_kernel,
        in_specs=[pl.BlockSpec(memory_space=SMEM)] + [pl.BlockSpec(memory_space=VMEM)] * 2,
        out_specs=pl.BlockSpec(memory_space=VMEM),
        out_shape=jax.ShapeDtypeStruct((rank, half), BF16),
        scratch_shapes=[VMEM((rank, half), F32)],
        compiler_params=params(8),
        name="finish",
    )(share, inverse, x)


def error_kernel(share_ref, *refs):
    mine, other = refs[:4], refs[4:8]
    pt_ref, merged_ref, q_ref, e_ref, qt_ref = refs[8:]
    k = pl.program_id(0)
    rank, half = mine[0].shape
    chip = share_ref[0] // 2
    core = lax.rem(share_ref[0], 2)

    @pl.when(k == 0)
    def _():
        for s in range(4):
            rows = pl.ds(pl.multiple_of((chip ^ s) * rank, rank), rank)
            for h in range(2):

                @pl.when(core == h)
                def _():
                    qt_ref[rows, h * half : (h + 1) * half] = mine[s][...]

                @pl.when(core != h)
                def _():
                    qt_ref[rows, h * half : (h + 1) * half] = other[s][...]

        q_ref[0] = qt_ref[...].T

    rows = pl.ds(pl.multiple_of(k * rank, rank), rank)
    p = pt_ref[rows, :].T
    hidden = merged_ref.shape[2]
    for n in range(0, hidden, 256):
        cols = pl.ds(n, 256)
        approx = dot(p, qt_ref[rows, cols], 1, 0)
        e_ref[0, 0, :, cols] = (merged_ref[0, :, cols].astype(F32) - approx).astype(BF16)


def error_of(share, mine, other, pt, merged):
    experts, rows, hidden = merged.shape
    width = pt.shape[0]
    whole = pl.BlockSpec(mine[0].shape, lambda k, share: (0, 0))
    return pl.pallas_call(
        error_kernel,
        grid_spec=pltpu.PrefetchScalarGridSpec(
            num_scalar_prefetch=1,
            grid=(experts,),
            in_specs=[whole] * 8
            + [
                pl.BlockSpec((width, rows), lambda k, share: (0, 0)),
                pl.BlockSpec((1, rows, hidden), lambda k, share: (k, 0, 0)),
            ],
            out_specs=[
                pl.BlockSpec((1, hidden, width), lambda k, share: (0, 0, 0)),
                pl.BlockSpec((1, 1, rows, hidden), lambda k, share: (0, k, 0, 0)),
            ],
            scratch_shapes=[VMEM((width, hidden), BF16)],
        ),
        out_shape=[
            jax.ShapeDtypeStruct((1, hidden, width), BF16),
            jax.ShapeDtypeStruct((1, experts, rows, hidden), BF16),
        ],
        compiler_params=params(BIG),
        name="error_of",
    )(share, *mine, *other, pt, merged)


def exchange(x, axis):
    return lax.all_to_all(x, axis, 0, 0, tiled=True)


def swap(x, bits):
    return lax.ppermute(x, "expert", [(i, i ^ bits) for i in range(lax.axis_size("expert"))])


def on_device(x_act, d_out, error, q_init, modality, membership):
    experts = x_act.shape[1]
    rank = q_init.shape[1] // experts
    replicas = membership.shape[0]
    share = lax.axis_index("expert").astype(jnp.int32).reshape(1)

    x_act, d_out, error, q_init = (
        pltpu.with_memory_space_constraint(a, pltpu.HBM) for a in (x_act, d_out, error, q_init)
    )
    merged, left = merge(x_act, d_out, error, q_init, replicas)
    merged = pltpu.with_memory_space_constraint(merged, pltpu.HBM)
    chunks = exchange(left, "dp")
    left_mean = exchange(mean_left(membership, modality, chunks), "dp")

    keep, send = raw_right(share, left_mean, merged)
    pieces = pair_sum(keep, swap(send, 1))
    pieces = [pieces[0]] + [swap(pieces[s], 2 * s) for s in (1, 2, 3)]
    columns = share_sum(pieces, replicas)

    columns, left_mean = lax.optimization_barrier((columns, left_mean))
    part = gram(left_mean, rank)
    part = part + swap(part, 1)
    grams = [part] + [swap(part, 2 * s) for s in (1, 2, 3)]
    columns, grams = lax.optimization_barrier((exchange(columns, "dp"), grams))
    means = mean_right(membership, modality, share, columns)
    pt, inverse = factor(grams, left_mean)
    own = finish(share, inverse, exchange(means, "dp"))
    mine = [own] + [swap(own, 2 * s) for s in (1, 2, 3)]
    other = [swap(piece, 1) for piece in mine]
    return tuple(error_of(share, mine, other, pt, merged))


def solution(mesh):
    in_specs = (
        P("dp", None, None, "expert"),
        P("dp", None, None, None),
        P("dp", None, "expert", None),
        P(),
        P(),
        P(),
    )
    out_specs = (P("dp", None, None), P("dp", None, "expert", None))
    return jax.shard_map(
        on_device, mesh=mesh, in_specs=in_specs, out_specs=out_specs, check_vma=False
    )
```

```python
import functools

import jax
import jax.numpy as jnp
from jax import lax
from jax.experimental import pallas as pl
from jax.experimental.pallas import tpu as pltpu
from jax.sharding import PartitionSpec as P

GROUPS = 4
F32 = jnp.float32
BF16 = jnp.bfloat16
HIGHEST = lax.Precision.HIGHEST
SMEM = pltpu.SMEM
VMEM = pltpu.VMEM
BIG = 58
HBM = pltpu.HBM
DMA = pltpu.SemaphoreType.DMA


def dot(a, b, ca, cb, precision=None):
    return lax.dot_general(
        a, b, (((ca,), (cb,)), ((), ())), precision=precision, preferred_element_type=F32
    )


def params(mib=40, **kw):
    return pltpu.CompilerParams(vmem_limit_bytes=mib << 20, **kw)


def fetch(source, target, sem):
    copy = pltpu.make_async_copy(source, target, sem)
    copy.start()
    return copy


def merge_kernel(
    x_hbm, d_hbm, e_hbm, q_hbm, merged_hbm, left_ref, x_ref, d_ref, e_ref, q_ref, m_ref, sems
):
    experts, rows, hidden = m_ref.shape
    rank = q_ref.shape[1] // experts
    loads = []
    for k in range(experts):
        loads.append(
            [
                fetch(x_hbm.at[0, k], x_ref.at[k], sems.at[0, k]),
                fetch(d_hbm.at[0, k], d_ref.at[k], sems.at[1, k]),
                fetch(e_hbm.at[0, k], e_ref.at[k], sems.at[2, k]),
            ]
        )
        if k == 0:
            loads[0].append(fetch(q_hbm, q_ref, sems.at[4, 0]))
    stores = []
    for k in range(experts):
        for copy in loads[k][:3]:
            copy.wait()
        xt = x_ref[k].T
        for n in range(0, hidden, 256):
            cols = slice(n, n + 256)
            grad = dot(xt, d_ref[k, :, cols], 1, 0)
            m_ref[k, :, cols] = (grad + e_ref[k, :, cols].astype(F32)).astype(BF16)
        stores.append(fetch(m_ref.at[k], merged_hbm.at[k], sems.at[3, k]))
        if k == 0:
            loads[0][3].wait()
        acc = dot(m_ref[k], q_ref[...], 1, 0).reshape(left_ref.shape)
        if k == 0:
            left_ref[...] = acc
        else:
            owner = lax.broadcasted_iota(jnp.int32, acc.shape, 2) // rank
            left_ref[...] = jnp.where(owner == k, acc, left_ref[...])
    for copy in stores:
        copy.wait()


def merge(x_act, d_out, error, q_init, parts):
    _, experts, tok, rows = x_act.shape
    hidden = d_out.shape[3]
    width = q_init.shape[1]
    return pl.pallas_call(
        merge_kernel,
        in_specs=[pl.BlockSpec(memory_space=HBM)] * 4,
        out_specs=[pl.BlockSpec(memory_space=HBM), pl.BlockSpec(memory_space=VMEM)],
        out_shape=[
            jax.ShapeDtypeStruct((experts, rows, hidden), BF16),
            jax.ShapeDtypeStruct((parts, rows // parts, width), F32),
        ],
        scratch_shapes=[
            VMEM((experts, tok, rows), BF16),
            VMEM((experts, tok, hidden), BF16),
            VMEM((experts, rows, hidden), BF16),
            VMEM((hidden, width), BF16),
            VMEM((experts, rows, hidden), BF16),
            DMA((5, experts)),
        ],
        compiler_params=params(BIG),
        name="merge",
    )(x_act, d_out, error, q_init)


def group_sums(member_ref, x_ref):
    replicas = x_ref.shape[0]
    sums = [jnp.zeros(x_ref.shape[1:], F32) for _ in range(GROUPS)]
    for j in range(replicas):
        v = x_ref[j]
        for g in range(GROUPS):
            sums[g] = sums[g] + jnp.where(member_ref[j] == g, v, 0.0)
    return sums


def mean_left_kernel(member_ref, mod_ref, x_ref, o_ref, g_ref):
    replicas, rows, width = x_ref.shape
    experts = mod_ref.shape[0]
    rank = width // experts
    sums = group_sums(member_ref, x_ref)
    whole = sums[0] + sums[1] + sums[2] + sums[3]
    owner = lax.broadcasted_iota(jnp.int32, (rows, width), 1) // rank
    image = jnp.zeros((rows, width), jnp.int32)
    for k in range(experts):
        flag = (mod_ref[k] == 0).astype(jnp.int32)
        image = jnp.where(owner == k, flag, image)
    for g in range(GROUPS):
        g_ref[g] = jnp.where(
            image == 1, whole * (1.0 / replicas), sums[g] * (GROUPS / replicas)
        )
    for j in range(replicas):
        o_ref[j] = g_ref[member_ref[j]]


def mean_left(membership, modality, x):
    return pl.pallas_call(
        mean_left_kernel,
        in_specs=[
            pl.BlockSpec(memory_space=SMEM),
            pl.BlockSpec(memory_space=SMEM),
            pl.BlockSpec(memory_space=VMEM),
        ],
        out_specs=pl.BlockSpec(memory_space=VMEM),
        out_shape=jax.ShapeDtypeStruct(x.shape, F32),
        scratch_shapes=[VMEM((GROUPS,) + x.shape[1:], F32)],
        compiler_params=params(8),
        name="mean_left",
    )(membership, modality, x)


def mean_right_kernel(member_ref, mod_ref, share_ref, x_ref, o_ref, g_ref):
    replicas = x_ref.shape[0]
    image = mod_ref[share_ref[0] // 2] == 0
    sums = group_sums(member_ref, x_ref)
    whole = sums[0] + sums[1] + sums[2] + sums[3]
    for g in range(GROUPS):
        g_ref[g] = jnp.where(image, whole * (1.0 / replicas), sums[g] * (GROUPS / replicas))
    for j in range(replicas):
        o_ref[j] = g_ref[member_ref[j]]


def mean_right(membership, modality, share, x):
    return pl.pallas_call(
        mean_right_kernel,
        in_specs=[pl.BlockSpec(memory_space=SMEM)] * 3 + [pl.BlockSpec(memory_space=VMEM)],
        out_specs=pl.BlockSpec(memory_space=VMEM),
        out_shape=jax.ShapeDtypeStruct(x.shape, F32),
        scratch_shapes=[VMEM((GROUPS,) + x.shape[1:], F32)],
        compiler_params=params(8),
        name="mean_right",
    )(membership, modality, share, x)


def inverse_factors(grams, inv_ref, rank):
    width = 2 * rank
    experts = grams.shape[1] // rank
    row = lax.broadcasted_iota(jnp.int32, (rank, width), 0)
    lane = lax.broadcasted_iota(jnp.int32, (rank, width), 1)
    eye = (row == lax.rem(lane, rank)).astype(F32)
    inv_ref[...] = jnp.zeros_like(inv_ref)
    systems = []
    for k in range(experts):
        pair = grams[:, (k // 2) * width : (k // 2 + 1) * width]
        turned = pltpu.roll(pair, rank, 1)
        mine = (lane >= rank) if k % 2 == 0 else (lane < rank)
        trace = jnp.sum(jnp.where(mine, turned * eye, 0.0), keepdims=True)
        shifted = turned + eye * (0.001 * trace / rank)
        systems.append(jnp.where(mine, shifted, eye))
    for j in range(rank):
        for k in range(experts):
            at = j + (rank if k % 2 == 0 else 0)
            m = systems[k]
            pivot_row = m[j : j + 1, :]
            pivot = pivot_row[:, at : at + 1]
            other = (lane[:1] < rank) if k % 2 == 0 else (lane[:1] >= rank)
            inv_ref[k * rank + j : k * rank + j + 1, (k // 2) * width : (k // 2 + 1) * width] = (
                jnp.where(other, pivot_row * lax.rsqrt(pivot), 0.0)
            )
            if j + 1 < rank:
                scaled = pivot_row * (1.0 / pivot)
                factor = jnp.where(row[:, :1] > j, m[:, at : at + 1], 0.0)
                systems[k] = m - factor * scaled


def raw_kernel(share_ref, left_ref, merged_hbm, keep_ref, send_ref, gram_ref, m_ref, sems):
    experts = m_ref.shape[0]
    loads = [fetch(merged_hbm.at[k], m_ref.at[k], sems.at[k]) for k in range(experts)]
    width = left_ref.shape[2]
    rank = width // experts
    half = keep_ref.shape[2]
    left = left_ref[...].reshape(-1, width)
    lt = left.T
    high = lt.astype(BF16)
    low = (lt - high.astype(F32)).astype(BF16)
    chip = share_ref[0] // 2
    core = lax.rem(share_ref[0], 2)
    for k in range(experts):
        rows = slice(k * rank, (k + 1) * rank)
        both = jnp.concatenate([high[rows], low[rows]], axis=0)
        loads[k].wait()
        for h in range(2):
            q = dot(both, m_ref[k, :, h * half : (h + 1) * half], 1, 0)
            q = q[:rank] + q[rank:]

            @pl.when(core == h)
            def _():
                keep_ref[k ^ chip] = q

            @pl.when(core != h)
            def _():
                send_ref[k ^ chip, :, :half] = q

    full = dot(lt, left, 1, 0, HIGHEST)
    for k in range(experts):
        block = slice(k * rank, (k + 1) * rank)
        gram_ref[:, block] = full[block, block]
    pair = send_ref.shape[2] - half
    for s in range(experts):
        at = (s % 2) * pair
        send_ref[s, :, half:] = gram_ref[:, at : at + pair]


def raw_right(share, left_mean, merged):
    experts, rows, hidden = merged.shape
    width = left_mean.shape[2]
    rank = width // experts
    half = hidden // 2
    return pl.pallas_call(
        raw_kernel,
        in_specs=[
            pl.BlockSpec(memory_space=SMEM),
            pl.BlockSpec(memory_space=VMEM),
            pl.BlockSpec(memory_space=HBM),
        ],
        out_specs=[pl.BlockSpec(memory_space=VMEM)] * 3,
        out_shape=[
            jax.ShapeDtypeStruct((experts, rank, half), F32),
            jax.ShapeDtypeStruct((experts, rank, half + width // 2), F32),
            jax.ShapeDtypeStruct((rank, width), F32),
        ],
        scratch_shapes=[VMEM(merged.shape, BF16), DMA((experts,))],
        compiler_params=params(50),
        name="raw_right",
    )(share, left_mean, merged)


def pair_sum_kernel(share_ref, keep_ref, got_ref, gram_ref, *o_refs):
    core = lax.rem(share_ref[0], 2)
    half = keep_ref.shape[2]
    pair = got_ref.shape[2] - half
    own = jnp.where(core == 0, gram_ref[:, :pair], gram_ref[:, pair:])
    other = jnp.where(core == 0, got_ref[0, :, half:], got_ref[1, :, half:])
    for s, o_ref in enumerate(o_refs):
        o_ref[:, :half] = keep_ref[s] + got_ref[s, :, :half]
        o_ref[:, half:] = own + other


def pair_sum(share, keep, got, gram):
    piece = jax.ShapeDtypeStruct(got.shape[1:], F32)
    return pl.pallas_call(
        pair_sum_kernel,
        in_specs=[pl.BlockSpec(memory_space=SMEM)] + [pl.BlockSpec(memory_space=VMEM)] * 3,
        out_specs=[pl.BlockSpec(memory_space=VMEM)] * got.shape[0],
        out_shape=[piece] * got.shape[0],
        compiler_params=params(8),
        name="pair_sum",
    )(share, keep, got, gram)


def share_sum_kernel(a_ref, b_ref, c_ref, d_ref, o_ref, gram_ref):
    total = (a_ref[...] + b_ref[...]) + (c_ref[...] + d_ref[...])
    replicas, tiles, lanes = o_ref.shape
    half = total.shape[1] - gram_ref.shape[1]
    across = half // lanes
    for t in range(tiles):
        r, c = divmod(t, across)
        o_ref[:, t, :] = total[r * replicas : (r + 1) * replicas, c * lanes : (c + 1) * lanes]
    gram_ref[...] = total[:, half:]


def share_sum(pieces, pair, replicas):
    rank, lanes = pieces[0].shape
    size = rank * (lanes - pair)
    return pl.pallas_call(
        share_sum_kernel,
        in_specs=[pl.BlockSpec(memory_space=VMEM)] * 4,
        out_specs=[pl.BlockSpec(memory_space=VMEM)] * 2,
        out_shape=[
            jax.ShapeDtypeStruct((replicas, size // (128 * replicas), 128), F32),
            jax.ShapeDtypeStruct((rank, pair), F32),
        ],
        compiler_params=params(8),
        name="share_sum",
    )(*pieces)


def factor_kernel(share_ref, own_ref, other_ref, left_ref, pt_ref, inverse_ref, inv_ref):
    experts, rank, _ = inverse_ref.shape
    first = lax.rem(share_ref[0], 2) == 0
    own, other = own_ref[...], other_ref[...]
    grams = jnp.concatenate([jnp.where(first, own, other), jnp.where(first, other, own)], axis=1)
    inverse_factors(grams, inv_ref, rank)
    left = left_ref[...].reshape(-1, left_ref.shape[2])
    pt_ref[...] = dot(inv_ref[...], left, 1, 1, HIGHEST).astype(BF16)
    for k in range(experts):
        block = slice(k * rank, (k + 1) * rank)
        inverse_ref[k] = inv_ref[block, block]


def factor(share, own, other, left_mean):
    rank, pair = own.shape
    width = 2 * pair
    replicas, rows, _ = left_mean.shape
    return pl.pallas_call(
        factor_kernel,
        in_specs=[pl.BlockSpec(memory_space=SMEM)] + [pl.BlockSpec(memory_space=VMEM)] * 3,
        out_specs=[pl.BlockSpec(memory_space=VMEM)] * 2,
        out_shape=[
            jax.ShapeDtypeStruct((width, replicas * rows), BF16),
            jax.ShapeDtypeStruct((width // rank, rank, rank), F32),
        ],
        scratch_shapes=[VMEM((width, width), F32)],
        compiler_params=params(8),
        cost_estimate=pl.CostEstimate(flops=1 << 30, bytes_accessed=1 << 20, transcendentals=0),
        name="factor",
    )(share, own, other, left_mean)


def finish_kernel(share_ref, inverse_ref, x_ref, o_ref, raw_ref):
    replicas, tiles, lanes = x_ref.shape
    across = raw_ref.shape[1] // lanes
    for t in range(tiles):
        r, c = divmod(t, across)
        raw_ref[r * replicas : (r + 1) * replicas, c * lanes : (c + 1) * lanes] = x_ref[:, t, :]
    inverse = inverse_ref[share_ref[0] // 2]
    o_ref[...] = dot(inverse, raw_ref[...], 1, 0, HIGHEST).astype(BF16)


def finish(share, inverse, x):
    rank = inverse.shape[1]
    half = x.size // rank
    return pl.pallas_call(
        finish_kernel,
        in_specs=[pl.BlockSpec(memory_space=SMEM)] + [pl.BlockSpec(memory_space=VMEM)] * 2,
        out_specs=pl.BlockSpec(memory_space=VMEM),
        out_shape=jax.ShapeDtypeStruct((rank, half), BF16),
        scratch_shapes=[VMEM((rank, half), F32)],
        compiler_params=params(8),
        name="finish",
    )(share, inverse, x)


def error_kernel(share_ref, *refs):
    mine, other = refs[:4], refs[4:8]
    pt_ref, merged_hbm, q_ref, e_hbm, qt_ref, m_ref, e_ref, sems = refs[8:]
    experts, _, hidden = m_ref.shape
    loads = [fetch(merged_hbm.at[k], m_ref.at[k], sems.at[0, k]) for k in range(experts)]
    rank, half = mine[0].shape
    chip = share_ref[0] // 2
    core = lax.rem(share_ref[0], 2)
    for s in range(4):
        rows = pl.ds(pl.multiple_of((chip ^ s) * rank, rank), rank)
        for h in range(2):

            @pl.when(core == h)
            def _():
                qt_ref[rows, h * half : (h + 1) * half] = mine[s][...]

            @pl.when(core != h)
            def _():
                qt_ref[rows, h * half : (h + 1) * half] = other[s][...]

    stores = []
    for k in range(experts):
        rows = slice(k * rank, (k + 1) * rank)
        p = pt_ref[rows, :].T
        loads[k].wait()
        for n in range(0, hidden, 256):
            cols = slice(n, n + 256)
            approx = dot(p, qt_ref[rows, cols], 1, 0)
            e_ref[k, :, cols] = (m_ref[k, :, cols].astype(F32) - approx).astype(BF16)
        stores.append(fetch(e_ref.at[k], e_hbm.at[0, k], sems.at[1, k]))
    q_ref[0] = qt_ref[...].T
    for copy in stores:
        copy.wait()


def error_of(share, mine, other, pt, merged):
    experts, rows, hidden = merged.shape
    width = pt.shape[0]
    return pl.pallas_call(
        error_kernel,
        in_specs=[pl.BlockSpec(memory_space=SMEM)]
        + [pl.BlockSpec(memory_space=VMEM)] * 9
        + [pl.BlockSpec(memory_space=HBM)],
        out_specs=[pl.BlockSpec(memory_space=VMEM), pl.BlockSpec(memory_space=HBM)],
        out_shape=[
            jax.ShapeDtypeStruct((1, hidden, width), BF16),
            jax.ShapeDtypeStruct((1, experts, rows, hidden), BF16),
        ],
        scratch_shapes=[
            VMEM((width, hidden), BF16),
            VMEM(merged.shape, BF16),
            VMEM(merged.shape, BF16),
            DMA((2, experts)),
        ],
        compiler_params=params(50),
        name="error_of",
    )(share, *mine, *other, pt, merged)


def exchange(x, axis):
    return lax.all_to_all(x, axis, 0, 0, tiled=True)


def swap(x, bits):
    return lax.ppermute(x, "expert", [(i, i ^ bits) for i in range(lax.axis_size("expert"))])


def on_device(x_act, d_out, error, q_init, modality, membership):
    experts = x_act.shape[1]
    rank = q_init.shape[1] // experts
    replicas = membership.shape[0]
    share = lax.axis_index("expert").astype(jnp.int32).reshape(1)

    merged, left = merge(x_act, d_out, error, q_init, replicas)
    chunks = exchange(left, "dp")
    left_mean = exchange(mean_left(membership, modality, chunks), "dp")

    keep, send, gram = raw_right(share, left_mean, merged)
    pieces = pair_sum(share, keep, swap(send, 1), gram)
    pieces = [pieces[0]] + [swap(pieces[s], 2 * s) for s in (1, 2, 3)]
    columns, gram = share_sum(pieces, 2 * rank, replicas)

    columns, gram = lax.optimization_barrier((exchange(columns, "dp"), gram))
    means = mean_right(membership, modality, share, columns)
    pt, inverse = factor(share, gram, swap(gram, 1), left_mean)
    own = finish(share, inverse, exchange(means, "dp"))
    mine = [own] + [swap(own, 2 * s) for s in (1, 2, 3)]
    other = [swap(piece, 1) for piece in mine]
    return tuple(error_of(share, mine, other, pt, merged))


def solution(mesh):
    in_specs = (
        P("dp", None, None, "expert"),
        P("dp", None, None, None),
        P("dp", None, "expert", None),
        P(),
        P(),
        P(),
    )
    out_specs = (P("dp", None, None), P("dp", None, "expert", None))
    return jax.shard_map(
        on_device, mesh=mesh, in_specs=in_specs, out_specs=out_specs, check_vma=False
    )
```

```python
import functools

import jax
import jax.numpy as jnp
from jax import lax
from jax.experimental import pallas as pl
from jax.experimental.pallas import tpu as pltpu
from jax.sharding import PartitionSpec as P

GROUPS = 4
F32 = jnp.float32
BF16 = jnp.bfloat16
HIGHEST = lax.Precision.HIGHEST
SMEM = pltpu.SMEM
VMEM = pltpu.VMEM
BIG = 56
HBM = pltpu.HBM
DMA = pltpu.SemaphoreType.DMA


def dot(a, b, ca, cb, precision=None):
    return lax.dot_general(
        a, b, (((ca,), (cb,)), ((), ())), precision=precision, preferred_element_type=F32
    )


def params(mib=40, **kw):
    return pltpu.CompilerParams(vmem_limit_bytes=mib << 20, **kw)


def fetch(source, target, sem):
    copy = pltpu.make_async_copy(source, target, sem)
    copy.start()
    return copy


def merge_kernel(
    x_hbm, d_hbm, e_hbm, q_hbm, merged_hbm, left_ref, x_ref, d_ref, e_ref, q_ref, m_ref, sems
):
    experts, rows, hidden = m_ref.shape
    rank = q_ref.shape[1] // experts
    loads = []
    for k in range(experts):
        loads.append(
            [
                fetch(x_hbm.at[0, k], x_ref.at[k], sems.at[0, k]),
                fetch(d_hbm.at[0, k], d_ref.at[k], sems.at[1, k]),
                fetch(e_hbm.at[0, k], e_ref.at[k], sems.at[2, k]),
            ]
        )
        if k == 0:
            loads[0].append(fetch(q_hbm, q_ref, sems.at[4, 0]))
    stores = []
    for k in range(experts):
        for copy in loads[k][:3]:
            copy.wait()
        xt = x_ref[k].T
        for n in range(0, hidden, 256):
            cols = slice(n, n + 256)
            grad = dot(xt, d_ref[k, :, cols], 1, 0)
            m_ref[k, :, cols] = (grad + e_ref[k, :, cols].astype(F32)).astype(BF16)
        stores.append(fetch(m_ref.at[k], merged_hbm.at[k], sems.at[3, k]))
        if k == 0:
            loads[0][3].wait()
        acc = dot(m_ref[k], q_ref[...], 1, 0).reshape(left_ref.shape)
        if k == 0:
            left_ref[...] = acc
        else:
            owner = lax.broadcasted_iota(jnp.int32, acc.shape, 2) // rank
            left_ref[...] = jnp.where(owner == k, acc, left_ref[...])
    for copy in stores:
        copy.wait()


def merge(x_act, d_out, error, q_init, parts):
    _, experts, tok, rows = x_act.shape
    hidden = d_out.shape[3]
    width = q_init.shape[1]
    return pl.pallas_call(
        merge_kernel,
        in_specs=[pl.BlockSpec(memory_space=HBM)] * 4,
        out_specs=[pl.BlockSpec(memory_space=HBM), pl.BlockSpec(memory_space=VMEM)],
        out_shape=[
            jax.ShapeDtypeStruct((experts, rows, hidden), BF16),
            jax.ShapeDtypeStruct((parts, rows // parts, width), F32),
        ],
        scratch_shapes=[
            VMEM((experts, tok, rows), BF16),
            VMEM((experts, tok, hidden), BF16),
            VMEM((experts, rows, hidden), BF16),
            VMEM((hidden, width), BF16),
            VMEM((experts, rows, hidden), BF16),
            DMA((5, experts)),
        ],
        compiler_params=params(BIG),
        name="merge",
    )(x_act, d_out, error, q_init)


def group_sums(member_ref, x_ref):
    replicas = x_ref.shape[0]
    sums = [jnp.zeros(x_ref.shape[1:], F32) for _ in range(GROUPS)]
    for j in range(replicas):
        v = x_ref[j]
        for g in range(GROUPS):
            sums[g] = sums[g] + jnp.where(member_ref[j] == g, v, 0.0)
    return sums


def mean_left_kernel(member_ref, mod_ref, x_ref, o_ref, g_ref):
    replicas, rows, width = x_ref.shape
    experts = mod_ref.shape[0]
    rank = width // experts
    sums = group_sums(member_ref, x_ref)
    whole = sums[0] + sums[1] + sums[2] + sums[3]
    owner = lax.broadcasted_iota(jnp.int32, (rows, width), 1) // rank
    image = jnp.zeros((rows, width), jnp.int32)
    for k in range(experts):
        flag = (mod_ref[k] == 0).astype(jnp.int32)
        image = jnp.where(owner == k, flag, image)
    for g in range(GROUPS):
        g_ref[g] = jnp.where(
            image == 1, whole * (1.0 / replicas), sums[g] * (GROUPS / replicas)
        )
    for j in range(replicas):
        o_ref[j] = g_ref[member_ref[j]]


def mean_left(membership, modality, x):
    return pl.pallas_call(
        mean_left_kernel,
        in_specs=[
            pl.BlockSpec(memory_space=SMEM),
            pl.BlockSpec(memory_space=SMEM),
            pl.BlockSpec(memory_space=VMEM),
        ],
        out_specs=pl.BlockSpec(memory_space=VMEM),
        out_shape=jax.ShapeDtypeStruct(x.shape, F32),
        scratch_shapes=[VMEM((GROUPS,) + x.shape[1:], F32)],
        compiler_params=params(8),
        name="mean_left",
    )(membership, modality, x)


def mean_right_kernel(member_ref, mod_ref, share_ref, x_ref, o_ref, g_ref):
    replicas = x_ref.shape[0]
    image = mod_ref[share_ref[0] // 2] == 0
    sums = group_sums(member_ref, x_ref)
    whole = sums[0] + sums[1] + sums[2] + sums[3]
    for g in range(GROUPS):
        g_ref[g] = jnp.where(image, whole * (1.0 / replicas), sums[g] * (GROUPS / replicas))
    for j in range(replicas):
        o_ref[j] = g_ref[member_ref[j]]


def mean_right(membership, modality, share, x):
    return pl.pallas_call(
        mean_right_kernel,
        in_specs=[pl.BlockSpec(memory_space=SMEM)] * 3 + [pl.BlockSpec(memory_space=VMEM)],
        out_specs=pl.BlockSpec(memory_space=VMEM),
        out_shape=jax.ShapeDtypeStruct(x.shape, F32),
        scratch_shapes=[VMEM((GROUPS,) + x.shape[1:], F32)],
        compiler_params=params(8),
        name="mean_right",
    )(membership, modality, share, x)


def inverse_factors(grams, inv_ref, rank):
    width = 2 * rank
    experts = grams.shape[1] // rank
    row = lax.broadcasted_iota(jnp.int32, (rank, width), 0)
    lane = lax.broadcasted_iota(jnp.int32, (rank, width), 1)
    eye = (row == lax.rem(lane, rank)).astype(F32)
    inv_ref[...] = jnp.zeros_like(inv_ref)
    systems = []
    for k in range(experts):
        pair = grams[:, (k // 2) * width : (k // 2 + 1) * width]
        turned = pltpu.roll(pair, rank, 1)
        mine = (lane >= rank) if k % 2 == 0 else (lane < rank)
        trace = jnp.sum(jnp.where(mine, turned * eye, 0.0), keepdims=True)
        shifted = turned + eye * (0.001 * trace / rank)
        systems.append(jnp.where(mine, shifted, eye))
    for j in range(rank):
        for k in range(experts):
            at = j + (rank if k % 2 == 0 else 0)
            m = systems[k]
            pivot_row = m[j : j + 1, :]
            pivot = pivot_row[:, at : at + 1]
            other = (lane[:1] < rank) if k % 2 == 0 else (lane[:1] >= rank)
            inv_ref[k * rank + j : k * rank + j + 1, (k // 2) * width : (k // 2 + 1) * width] = (
                jnp.where(other, pivot_row * lax.rsqrt(pivot), 0.0)
            )
            if j + 1 < rank:
                scaled = pivot_row * (1.0 / pivot)
                factor = jnp.where(row[:, :1] > j, m[:, at : at + 1], 0.0)
                systems[k] = m - factor * scaled


def raw_kernel(share_ref, left_ref, merged_hbm, keep_ref, send_ref, gram_ref, m_ref, sems):
    experts = m_ref.shape[0]
    loads = [fetch(merged_hbm.at[k], m_ref.at[k], sems.at[k]) for k in range(experts)]
    width = left_ref.shape[2]
    rank = width // experts
    half = keep_ref.shape[2]
    left = left_ref[...].reshape(-1, width)
    lt = left.T
    high = lt.astype(BF16)
    low = (lt - high.astype(F32)).astype(BF16)
    full = dot(lt, left, 1, 0, HIGHEST)
    for k in range(experts):
        block = slice(k * rank, (k + 1) * rank)
        gram_ref[:, block] = full[block, block]
    pair = send_ref.shape[2] - half
    for s in range(experts):
        at = (s % 2) * pair
        send_ref[s, :, half:] = gram_ref[:, at : at + pair]
    chip = share_ref[0] // 2
    core = lax.rem(share_ref[0], 2)
    for k in range(experts):
        rows = slice(k * rank, (k + 1) * rank)
        both = jnp.concatenate([high[rows], low[rows]], axis=0)
        loads[k].wait()
        for h in range(2):
            q = dot(both, m_ref[k, :, h * half : (h + 1) * half], 1, 0)
            q = q[:rank] + q[rank:]

            @pl.when(core == h)
            def _():
                keep_ref[k ^ chip] = q

            @pl.when(core != h)
            def _():
                send_ref[k ^ chip, :, :half] = q


def raw_right(share, left_mean, merged):
    experts, rows, hidden = merged.shape
    width = left_mean.shape[2]
    rank = width // experts
    half = hidden // 2
    return pl.pallas_call(
        raw_kernel,
        in_specs=[
            pl.BlockSpec(memory_space=SMEM),
            pl.BlockSpec(memory_space=VMEM),
            pl.BlockSpec(memory_space=HBM),
        ],
        out_specs=[pl.BlockSpec(memory_space=VMEM)] * 3,
        out_shape=[
            jax.ShapeDtypeStruct((experts, rank, half), F32),
            jax.ShapeDtypeStruct((experts, rank, half + width // 2), F32),
            jax.ShapeDtypeStruct((rank, width), F32),
        ],
        scratch_shapes=[VMEM(merged.shape, BF16), DMA((experts,))],
        compiler_params=params(50),
        name="raw_right",
    )(share, left_mean, merged)


def pair_sum_kernel(share_ref, keep_ref, got_ref, gram_ref, *o_refs):
    core = lax.rem(share_ref[0], 2)
    half = keep_ref.shape[2]
    pair = got_ref.shape[2] - half
    own = jnp.where(core == 0, gram_ref[:, :pair], gram_ref[:, pair:])
    other = jnp.where(core == 0, got_ref[0, :, half:], got_ref[1, :, half:])
    for s, o_ref in enumerate(o_refs):
        o_ref[:, :half] = keep_ref[s] + got_ref[s, :, :half]
        o_ref[:, half:] = own + other


def pair_sum(share, keep, got, gram):
    piece = jax.ShapeDtypeStruct(got.shape[1:], F32)
    return pl.pallas_call(
        pair_sum_kernel,
        in_specs=[pl.BlockSpec(memory_space=SMEM)] + [pl.BlockSpec(memory_space=VMEM)] * 3,
        out_specs=[pl.BlockSpec(memory_space=VMEM)] * got.shape[0],
        out_shape=[piece] * got.shape[0],
        compiler_params=params(8),
        name="pair_sum",
    )(share, keep, got, gram)


def share_sum_kernel(a_ref, b_ref, c_ref, d_ref, o_ref, gram_ref):
    total = (a_ref[...] + b_ref[...]) + (c_ref[...] + d_ref[...])
    replicas, tiles, lanes = o_ref.shape
    half = total.shape[1] - gram_ref.shape[1]
    across = half // lanes
    for t in range(tiles):
        r, c = divmod(t, across)
        o_ref[:, t, :] = total[r * replicas : (r + 1) * replicas, c * lanes : (c + 1) * lanes]
    gram_ref[...] = total[:, half:]


def share_sum(pieces, pair, replicas):
    rank, lanes = pieces[0].shape
    size = rank * (lanes - pair)
    return pl.pallas_call(
        share_sum_kernel,
        in_specs=[pl.BlockSpec(memory_space=VMEM)] * 4,
        out_specs=[pl.BlockSpec(memory_space=VMEM)] * 2,
        out_shape=[
            jax.ShapeDtypeStruct((replicas, size // (128 * replicas), 128), F32),
            jax.ShapeDtypeStruct((rank, pair), F32),
        ],
        compiler_params=params(8),
        name="share_sum",
    )(*pieces)


def factor_kernel(share_ref, own_ref, other_ref, left_ref, pt_ref, inverse_ref, inv_ref):
    experts, rank, _ = inverse_ref.shape
    first = lax.rem(share_ref[0], 2) == 0
    own, other = own_ref[...], other_ref[...]
    grams = jnp.concatenate([jnp.where(first, own, other), jnp.where(first, other, own)], axis=1)
    inverse_factors(grams, inv_ref, rank)
    left = left_ref[...].reshape(-1, left_ref.shape[2])
    pt_ref[...] = dot(inv_ref[...], left, 1, 1, HIGHEST).astype(BF16)
    for k in range(experts):
        block = slice(k * rank, (k + 1) * rank)
        inverse_ref[k] = inv_ref[block, block]


def factor(share, own, other, left_mean):
    rank, pair = own.shape
    width = 2 * pair
    replicas, rows, _ = left_mean.shape
    return pl.pallas_call(
        factor_kernel,
        in_specs=[pl.BlockSpec(memory_space=SMEM)] + [pl.BlockSpec(memory_space=VMEM)] * 3,
        out_specs=[pl.BlockSpec(memory_space=VMEM)] * 2,
        out_shape=[
            jax.ShapeDtypeStruct((width, replicas * rows), BF16),
            jax.ShapeDtypeStruct((width // rank, rank, rank), F32),
        ],
        scratch_shapes=[VMEM((width, width), F32)],
        compiler_params=params(8),
        cost_estimate=pl.CostEstimate(flops=1 << 30, bytes_accessed=1 << 20, transcendentals=0),
        name="factor",
    )(share, own, other, left_mean)


def finish_kernel(share_ref, inverse_ref, x_ref, o_ref, raw_ref):
    replicas, tiles, lanes = x_ref.shape
    across = raw_ref.shape[1] // lanes
    for t in range(tiles):
        r, c = divmod(t, across)
        raw_ref[r * replicas : (r + 1) * replicas, c * lanes : (c + 1) * lanes] = x_ref[:, t, :]
    inverse = inverse_ref[share_ref[0] // 2]
    o_ref[...] = dot(inverse, raw_ref[...], 1, 0, HIGHEST).astype(BF16)


def finish(share, inverse, x):
    rank = inverse.shape[1]
    half = x.size // rank
    return pl.pallas_call(
        finish_kernel,
        in_specs=[pl.BlockSpec(memory_space=SMEM)] + [pl.BlockSpec(memory_space=VMEM)] * 2,
        out_specs=pl.BlockSpec(memory_space=VMEM),
        out_shape=jax.ShapeDtypeStruct((rank, half), BF16),
        scratch_shapes=[VMEM((rank, half), F32)],
        compiler_params=params(8),
        name="finish",
    )(share, inverse, x)


def error_kernel(share_ref, *refs):
    mine, other = refs[:4], refs[4:8]
    pt_ref, merged_hbm, q_hbm, e_hbm, qt_ref, m_ref, e_ref, q_ref, sems = refs[8:]
    experts, _, hidden = m_ref.shape
    loads = [fetch(merged_hbm.at[k], m_ref.at[k], sems.at[0, k]) for k in range(experts)]
    rank, half = mine[0].shape
    chip = share_ref[0] // 2
    core = lax.rem(share_ref[0], 2)
    for s in range(4):
        rows = pl.ds(pl.multiple_of((chip ^ s) * rank, rank), rank)
        for h in range(2):

            @pl.when(core == h)
            def _():
                qt_ref[rows, h * half : (h + 1) * half] = mine[s][...]

            @pl.when(core != h)
            def _():
                qt_ref[rows, h * half : (h + 1) * half] = other[s][...]

    q_ref[...] = qt_ref[...].T
    stores = [fetch(q_ref, q_hbm.at[0], sems.at[2, 0])]
    for k in range(experts):
        rows = slice(k * rank, (k + 1) * rank)
        p = pt_ref[rows, :].T
        loads[k].wait()
        for n in range(0, hidden, 256):
            cols = slice(n, n + 256)
            approx = dot(p, qt_ref[rows, cols], 1, 0)
            e_ref[k, :, cols] = (m_ref[k, :, cols].astype(F32) - approx).astype(BF16)
        stores.append(fetch(e_ref.at[k], e_hbm.at[0, k], sems.at[1, k]))
    for copy in stores:
        copy.wait()


def error_of(share, mine, other, pt, merged):
    experts, rows, hidden = merged.shape
    width = pt.shape[0]
    return pl.pallas_call(
        error_kernel,
        in_specs=[pl.BlockSpec(memory_space=SMEM)]
        + [pl.BlockSpec(memory_space=VMEM)] * 9
        + [pl.BlockSpec(memory_space=HBM)],
        out_specs=[pl.BlockSpec(memory_space=HBM)] * 2,
        out_shape=[
            jax.ShapeDtypeStruct((1, hidden, width), BF16),
            jax.ShapeDtypeStruct((1, experts, rows, hidden), BF16),
        ],
        scratch_shapes=[
            VMEM((width, hidden), BF16),
            VMEM(merged.shape, BF16),
            VMEM(merged.shape, BF16),
            VMEM((hidden, width), BF16),
            DMA((3, experts)),
        ],
        compiler_params=params(50),
        name="error_of",
    )(share, *mine, *other, pt, merged)


def exchange(x, axis):
    return lax.all_to_all(x, axis, 0, 0, tiled=True)


def swap(x, bits):
    return lax.ppermute(x, "expert", [(i, i ^ bits) for i in range(lax.axis_size("expert"))])


def on_device(x_act, d_out, error, q_init, modality, membership):
    experts = x_act.shape[1]
    rank = q_init.shape[1] // experts
    replicas = membership.shape[0]
    share = lax.axis_index("expert").astype(jnp.int32).reshape(1)

    x_act, d_out, error, q_init = (
        pltpu.with_memory_space_constraint(a, HBM) for a in (x_act, d_out, error, q_init)
    )
    q_init, share = lax.optimization_barrier((q_init, share))
    merged, left = merge(x_act, d_out, error, q_init, replicas)
    chunks = exchange(left, "dp")
    left_mean = exchange(mean_left(membership, modality, chunks), "dp")

    keep, send, gram = raw_right(share, left_mean, merged)
    pieces = pair_sum(share, keep, swap(send, 1), gram)
    pieces = [pieces[0]] + [swap(pieces[s], 2 * s) for s in (1, 2, 3)]
    columns, gram = share_sum(pieces, 2 * rank, replicas)

    columns, gram = lax.optimization_barrier((exchange(columns, "dp"), gram))
    means = mean_right(membership, modality, share, columns)
    pt, inverse = factor(share, gram, swap(gram, 1), left_mean)
    own = finish(share, inverse, exchange(means, "dp"))
    mine = [own] + [swap(own, 2 * s) for s in (1, 2, 3)]
    other = [swap(piece, 1) for piece in mine]
    return tuple(error_of(share, mine, other, pt, merged))


def solution(mesh):
    in_specs = (
        P("dp", None, None, "expert"),
        P("dp", None, None, None),
        P("dp", None, "expert", None),
        P(),
        P(),
        P(),
    )
    out_specs = (P("dp", None, None), P("dp", None, "expert", None))
    return jax.shard_map(
        on_device, mesh=mesh, in_specs=in_specs, out_specs=out_specs, check_vma=False
    )
```

```python
import functools

import jax
import jax.numpy as jnp
from jax import lax
from jax.experimental import pallas as pl
from jax.experimental.pallas import tpu as pltpu
from jax.sharding import PartitionSpec as P

GROUPS = 4
F32 = jnp.float32
BF16 = jnp.bfloat16
HIGHEST = lax.Precision.HIGHEST
SMEM = pltpu.SMEM
VMEM = pltpu.VMEM
BIG = 56
HBM = pltpu.HBM
DMA = pltpu.SemaphoreType.DMA


def dot(a, b, ca, cb, precision=None):
    return lax.dot_general(
        a, b, (((ca,), (cb,)), ((), ())), precision=precision, preferred_element_type=F32
    )


def params(mib=40, **kw):
    return pltpu.CompilerParams(vmem_limit_bytes=mib << 20, **kw)


def fetch(source, target, sem):
    copy = pltpu.make_async_copy(source, target, sem)
    copy.start()
    return copy


def merge_kernel(
    x_hbm, d_hbm, e_hbm, q_hbm, merged_hbm, left_ref, x_ref, d_ref, e_ref, q_ref, m_ref, sems
):
    experts, rows, hidden = m_ref.shape
    rank = q_ref.shape[1] // experts
    loads = []
    for k in range(experts):
        loads.append(
            [
                fetch(x_hbm.at[0, k], x_ref.at[k], sems.at[0, k]),
                fetch(d_hbm.at[0, k], d_ref.at[k], sems.at[1, k]),
                fetch(e_hbm.at[0, k], e_ref.at[k], sems.at[2, k]),
            ]
        )
        if k == 0:
            loads[0].append(fetch(q_hbm, q_ref, sems.at[4, 0]))
    stores = []
    for k in range(experts):
        for copy in loads[k][:3]:
            copy.wait()
        xt = x_ref[k].T
        for n in range(0, hidden, 256):
            cols = slice(n, n + 256)
            grad = dot(xt, d_ref[k, :, cols], 1, 0)
            m_ref[k, :, cols] = (grad + e_ref[k, :, cols].astype(F32)).astype(BF16)
        stores.append(fetch(m_ref.at[k], merged_hbm.at[k], sems.at[3, k]))
        if k == 0:
            loads[0][3].wait()
        acc = dot(m_ref[k], q_ref[...], 1, 0).reshape(left_ref.shape)
        if k == 0:
            left_ref[...] = acc
        else:
            owner = lax.broadcasted_iota(jnp.int32, acc.shape, 2) // rank
            left_ref[...] = jnp.where(owner == k, acc, left_ref[...])
    for copy in stores:
        copy.wait()


def merge(x_act, d_out, error, q_init, parts):
    _, experts, tok, rows = x_act.shape
    hidden = d_out.shape[3]
    width = q_init.shape[1]
    return pl.pallas_call(
        merge_kernel,
        in_specs=[pl.BlockSpec(memory_space=HBM)] * 4,
        out_specs=[pl.BlockSpec(memory_space=HBM), pl.BlockSpec(memory_space=VMEM)],
        out_shape=[
            jax.ShapeDtypeStruct((experts, rows, hidden), BF16),
            jax.ShapeDtypeStruct((parts, rows // parts, width), F32),
        ],
        scratch_shapes=[
            VMEM((experts, tok, rows), BF16),
            VMEM((experts, tok, hidden), BF16),
            VMEM((experts, rows, hidden), BF16),
            VMEM((hidden, width), BF16),
            VMEM((experts, rows, hidden), BF16),
            DMA((5, experts)),
        ],
        compiler_params=params(BIG),
        name="merge",
    )(x_act, d_out, error, q_init)


def group_sums(member_ref, x_ref):
    replicas = x_ref.shape[0]
    sums = [jnp.zeros(x_ref.shape[1:], F32) for _ in range(GROUPS)]
    for j in range(replicas):
        v = x_ref[j]
        for g in range(GROUPS):
            sums[g] = sums[g] + jnp.where(member_ref[j] == g, v, 0.0)
    return sums


def mean_left_kernel(member_ref, mod_ref, x_ref, o_ref, g_ref):
    replicas, rows, width = x_ref.shape
    experts = mod_ref.shape[0]
    rank = width // experts
    sums = group_sums(member_ref, x_ref)
    whole = sums[0] + sums[1] + sums[2] + sums[3]
    owner = lax.broadcasted_iota(jnp.int32, (rows, width), 1) // rank
    image = jnp.zeros((rows, width), jnp.int32)
    for k in range(experts):
        flag = (mod_ref[k] == 0).astype(jnp.int32)
        image = jnp.where(owner == k, flag, image)
    for g in range(GROUPS):
        g_ref[g] = jnp.where(
            image == 1, whole * (1.0 / replicas), sums[g] * (GROUPS / replicas)
        )
    for j in range(replicas):
        o_ref[j] = g_ref[member_ref[j]]


def mean_left(membership, modality, x):
    return pl.pallas_call(
        mean_left_kernel,
        in_specs=[
            pl.BlockSpec(memory_space=SMEM),
            pl.BlockSpec(memory_space=SMEM),
            pl.BlockSpec(memory_space=VMEM),
        ],
        out_specs=pl.BlockSpec(memory_space=VMEM),
        out_shape=jax.ShapeDtypeStruct(x.shape, F32),
        scratch_shapes=[VMEM((GROUPS,) + x.shape[1:], F32)],
        compiler_params=params(8),
        name="mean_left",
    )(membership, modality, x)


def mean_right_kernel(member_ref, mod_ref, share_ref, x_ref, o_ref, g_ref):
    replicas = x_ref.shape[0]
    image = mod_ref[share_ref[0] // 2] == 0
    sums = group_sums(member_ref, x_ref)
    whole = sums[0] + sums[1] + sums[2] + sums[3]
    for g in range(GROUPS):
        g_ref[g] = jnp.where(image, whole * (1.0 / replicas), sums[g] * (GROUPS / replicas))
    for j in range(replicas):
        o_ref[j] = g_ref[member_ref[j]]


def mean_right(membership, modality, share, x):
    return pl.pallas_call(
        mean_right_kernel,
        in_specs=[pl.BlockSpec(memory_space=SMEM)] * 3 + [pl.BlockSpec(memory_space=VMEM)],
        out_specs=pl.BlockSpec(memory_space=VMEM),
        out_shape=jax.ShapeDtypeStruct(x.shape, F32),
        scratch_shapes=[VMEM((GROUPS,) + x.shape[1:], F32)],
        compiler_params=params(8),
        name="mean_right",
    )(membership, modality, share, x)


def inverse_factors(grams, inv_ref, rank):
    width = 2 * rank
    experts = grams.shape[1] // rank
    row = lax.broadcasted_iota(jnp.int32, (rank, width), 0)
    lane = lax.broadcasted_iota(jnp.int32, (rank, width), 1)
    eye = (row == lax.rem(lane, rank)).astype(F32)
    inv_ref[...] = jnp.zeros_like(inv_ref)
    systems = []
    for k in range(experts):
        pair = grams[:, (k // 2) * width : (k // 2 + 1) * width]
        turned = pltpu.roll(pair, rank, 1)
        mine = (lane >= rank) if k % 2 == 0 else (lane < rank)
        trace = jnp.sum(jnp.where(mine, turned * eye, 0.0), keepdims=True)
        shifted = turned + eye * (0.001 * trace / rank)
        systems.append(jnp.where(mine, shifted, eye))
    for j in range(rank):
        base, local = j - j % 8, j % 8
        for k in range(experts):
            at = j + (rank if k % 2 == 0 else 0)
            m = systems[k] if local or j == 0 else systems[k][8:]
            pivot_row = m[local : local + 1, :]
            pivot = pivot_row[:, at : at + 1]
            other = (lane[:1] < rank) if k % 2 == 0 else (lane[:1] >= rank)
            inv_ref[k * rank + j : k * rank + j + 1, (k // 2) * width : (k // 2 + 1) * width] = (
                jnp.where(other, pivot_row * lax.rsqrt(pivot), 0.0)
            )
            if j + 1 < rank:
                scaled = pivot_row * (1.0 / pivot)
                factor = jnp.where(row[: rank - base, :1] > local, m[:, at : at + 1], 0.0)
                systems[k] = m - factor * scaled


def raw_kernel(share_ref, left_ref, merged_hbm, keep_ref, send_ref, gram_ref, m_ref, sems):
    experts = m_ref.shape[0]
    loads = [fetch(merged_hbm.at[k], m_ref.at[k], sems.at[k]) for k in range(experts)]
    width = left_ref.shape[2]
    rank = width // experts
    half = keep_ref.shape[2]
    left = left_ref[...].reshape(-1, width)
    lt = left.T
    high = lt.astype(BF16)
    low = (lt - high.astype(F32)).astype(BF16)
    full = dot(lt, left, 1, 0, HIGHEST)
    for k in range(experts):
        block = slice(k * rank, (k + 1) * rank)
        gram_ref[:, block] = full[block, block]
    pair = send_ref.shape[2] - half
    for s in range(experts):
        at = (s % 2) * pair
        send_ref[s, :, half:] = gram_ref[:, at : at + pair]
    chip = share_ref[0] // 2
    core = lax.rem(share_ref[0], 2)
    for k in range(experts):
        rows = slice(k * rank, (k + 1) * rank)
        both = jnp.concatenate([high[rows], low[rows]], axis=0)
        loads[k].wait()
        for h in range(2):
            q = dot(both, m_ref[k, :, h * half : (h + 1) * half], 1, 0)
            q = q[:rank] + q[rank:]

            @pl.when(core == h)
            def _():
                keep_ref[k ^ chip] = q

            @pl.when(core != h)
            def _():
                send_ref[k ^ chip, :, :half] = q


def raw_right(share, left_mean, merged):
    experts, rows, hidden = merged.shape
    width = left_mean.shape[2]
    rank = width // experts
    half = hidden // 2
    return pl.pallas_call(
        raw_kernel,
        in_specs=[
            pl.BlockSpec(memory_space=SMEM),
            pl.BlockSpec(memory_space=VMEM),
            pl.BlockSpec(memory_space=HBM),
        ],
        out_specs=[pl.BlockSpec(memory_space=VMEM)] * 3,
        out_shape=[
            jax.ShapeDtypeStruct((experts, rank, half), F32),
            jax.ShapeDtypeStruct((experts, rank, half + width // 2), F32),
            jax.ShapeDtypeStruct((rank, width), F32),
        ],
        scratch_shapes=[VMEM(merged.shape, BF16), DMA((experts,))],
        compiler_params=params(50),
        name="raw_right",
    )(share, left_mean, merged)


def pair_sum_kernel(share_ref, keep_ref, got_ref, gram_ref, *o_refs):
    core = lax.rem(share_ref[0], 2)
    half = keep_ref.shape[2]
    pair = got_ref.shape[2] - half
    own = jnp.where(core == 0, gram_ref[:, :pair], gram_ref[:, pair:])
    other = jnp.where(core == 0, got_ref[0, :, half:], got_ref[1, :, half:])
    for s, o_ref in enumerate(o_refs):
        o_ref[:, :half] = keep_ref[s] + got_ref[s, :, :half]
        o_ref[:, half:] = own + other


def pair_sum(share, keep, got, gram):
    piece = jax.ShapeDtypeStruct(got.shape[1:], F32)
    return pl.pallas_call(
        pair_sum_kernel,
        in_specs=[pl.BlockSpec(memory_space=SMEM)] + [pl.BlockSpec(memory_space=VMEM)] * 3,
        out_specs=[pl.BlockSpec(memory_space=VMEM)] * got.shape[0],
        out_shape=[piece] * got.shape[0],
        compiler_params=params(8),
        name="pair_sum",
    )(share, keep, got, gram)


def share_sum_kernel(a_ref, b_ref, c_ref, d_ref, o_ref, gram_ref):
    total = (a_ref[...] + b_ref[...]) + (c_ref[...] + d_ref[...])
    replicas, tiles, lanes = o_ref.shape
    half = total.shape[1] - gram_ref.shape[1]
    across = half // lanes
    for t in range(tiles):
        r, c = divmod(t, across)
        o_ref[:, t, :] = total[r * replicas : (r + 1) * replicas, c * lanes : (c + 1) * lanes]
    gram_ref[...] = total[:, half:]


def share_sum(pieces, pair, replicas):
    rank, lanes = pieces[0].shape
    size = rank * (lanes - pair)
    return pl.pallas_call(
        share_sum_kernel,
        in_specs=[pl.BlockSpec(memory_space=VMEM)] * 4,
        out_specs=[pl.BlockSpec(memory_space=VMEM)] * 2,
        out_shape=[
            jax.ShapeDtypeStruct((replicas, size // (128 * replicas), 128), F32),
            jax.ShapeDtypeStruct((rank, pair), F32),
        ],
        compiler_params=params(8),
        name="share_sum",
    )(*pieces)


def factor_kernel(share_ref, own_ref, other_ref, inverse_ref, inv_ref):
    experts, rank, _ = inverse_ref.shape
    first = lax.rem(share_ref[0], 2) == 0
    own, other = own_ref[...], other_ref[...]
    grams = jnp.concatenate([jnp.where(first, own, other), jnp.where(first, other, own)], axis=1)
    inverse_factors(grams, inv_ref, rank)
    for k in range(experts):
        block = slice(k * rank, (k + 1) * rank)
        inverse_ref[k] = inv_ref[block, block]


def factor(share, own, other):
    rank, pair = own.shape
    width = 2 * pair
    return pl.pallas_call(
        factor_kernel,
        in_specs=[pl.BlockSpec(memory_space=SMEM)] + [pl.BlockSpec(memory_space=VMEM)] * 2,
        out_specs=[pl.BlockSpec(memory_space=VMEM)] * 2,
        out_shape=[
            jax.ShapeDtypeStruct((width // rank, rank, rank), F32),
            jax.ShapeDtypeStruct((width, width), F32),
        ],
        compiler_params=params(8),
        cost_estimate=pl.CostEstimate(flops=1 << 30, bytes_accessed=1 << 20, transcendentals=0),
        name="factor",
    )(share, own, other)


def orthonormal_kernel(inv_ref, left_ref, pt_ref):
    left = left_ref[...].reshape(-1, left_ref.shape[2])
    pt_ref[...] = dot(inv_ref[...], left, 1, 1, HIGHEST).astype(BF16)


def orthonormal(inverse, left_mean):
    replicas, rows, width = left_mean.shape
    return pl.pallas_call(
        orthonormal_kernel,
        in_specs=[pl.BlockSpec(memory_space=VMEM)] * 2,
        out_specs=pl.BlockSpec(memory_space=VMEM),
        out_shape=jax.ShapeDtypeStruct((width, replicas * rows), BF16),
        compiler_params=params(8),
        cost_estimate=pl.CostEstimate(flops=1 << 29, bytes_accessed=1 << 20, transcendentals=0),
        name="orthonormal",
    )(inverse, left_mean)


def finish_kernel(share_ref, inverse_ref, x_ref, o_ref, raw_ref):
    replicas, tiles, lanes = x_ref.shape
    across = raw_ref.shape[1] // lanes
    for t in range(tiles):
        r, c = divmod(t, across)
        raw_ref[r * replicas : (r + 1) * replicas, c * lanes : (c + 1) * lanes] = x_ref[:, t, :]
    inverse = inverse_ref[share_ref[0] // 2]
    o_ref[...] = dot(inverse, raw_ref[...], 1, 0, HIGHEST).astype(BF16)


def finish(share, inverse, x):
    rank = inverse.shape[1]
    half = x.size // rank
    return pl.pallas_call(
        finish_kernel,
        in_specs=[pl.BlockSpec(memory_space=SMEM)] + [pl.BlockSpec(memory_space=VMEM)] * 2,
        out_specs=pl.BlockSpec(memory_space=VMEM),
        out_shape=jax.ShapeDtypeStruct((rank, half), BF16),
        scratch_shapes=[VMEM((rank, half), F32)],
        compiler_params=params(8),
        name="finish",
    )(share, inverse, x)


def error_kernel(share_ref, *refs):
    mine, other = refs[:4], refs[4:8]
    pt_ref, merged_hbm, q_hbm, e_hbm, qt_ref, m_ref, e_ref, q_ref, sems = refs[8:]
    experts, _, hidden = m_ref.shape
    loads = [fetch(merged_hbm.at[k], m_ref.at[k], sems.at[0, k]) for k in range(experts)]
    rank, half = mine[0].shape
    chip = share_ref[0] // 2
    core = lax.rem(share_ref[0], 2)
    for s in range(4):
        rows = pl.ds(pl.multiple_of((chip ^ s) * rank, rank), rank)
        for h in range(2):

            @pl.when(core == h)
            def _():
                qt_ref[rows, h * half : (h + 1) * half] = mine[s][...]

            @pl.when(core != h)
            def _():
                qt_ref[rows, h * half : (h + 1) * half] = other[s][...]

    q_ref[...] = qt_ref[...].T
    stores = [fetch(q_ref, q_hbm.at[0], sems.at[2, 0])]
    for k in range(experts):
        rows = slice(k * rank, (k + 1) * rank)
        p = pt_ref[rows, :].T
        loads[k].wait()
        for n in range(0, hidden, 256):
            cols = slice(n, n + 256)
            approx = dot(p, qt_ref[rows, cols], 1, 0)
            e_ref[k, :, cols] = (m_ref[k, :, cols].astype(F32) - approx).astype(BF16)
        stores.append(fetch(e_ref.at[k], e_hbm.at[0, k], sems.at[1, k]))
    for copy in stores:
        copy.wait()


def error_of(share, mine, other, pt, merged):
    experts, rows, hidden = merged.shape
    width = pt.shape[0]
    return pl.pallas_call(
        error_kernel,
        in_specs=[pl.BlockSpec(memory_space=SMEM)]
        + [pl.BlockSpec(memory_space=VMEM)] * 9
        + [pl.BlockSpec(memory_space=HBM)],
        out_specs=[pl.BlockSpec(memory_space=HBM)] * 2,
        out_shape=[
            jax.ShapeDtypeStruct((1, hidden, width), BF16),
            jax.ShapeDtypeStruct((1, experts, rows, hidden), BF16),
        ],
        scratch_shapes=[
            VMEM((width, hidden), BF16),
            VMEM(merged.shape, BF16),
            VMEM(merged.shape, BF16),
            VMEM((hidden, width), BF16),
            DMA((3, experts)),
        ],
        compiler_params=params(50),
        name="error_of",
    )(share, *mine, *other, pt, merged)


def exchange(x, axis):
    return lax.all_to_all(x, axis, 0, 0, tiled=True)


def swap(x, bits):
    return lax.ppermute(x, "expert", [(i, i ^ bits) for i in range(lax.axis_size("expert"))])


def on_device(x_act, d_out, error, q_init, modality, membership):
    experts = x_act.shape[1]
    rank = q_init.shape[1] // experts
    replicas = membership.shape[0]
    share = lax.axis_index("expert").astype(jnp.int32).reshape(1)

    x_act, d_out, error, q_init = (
        pltpu.with_memory_space_constraint(a, HBM) for a in (x_act, d_out, error, q_init)
    )
    q_init, share = lax.optimization_barrier((q_init, share))
    merged, left = merge(x_act, d_out, error, q_init, replicas)
    chunks = exchange(left, "dp")
    left_mean = exchange(mean_left(membership, modality, chunks), "dp")

    keep, send, gram = raw_right(share, left_mean, merged)
    pieces = pair_sum(share, keep, swap(send, 1), gram)
    pieces = [pieces[0]] + [swap(pieces[s], 2 * s) for s in (1, 2, 3)]
    columns, gram = share_sum(pieces, 2 * rank, replicas)

    columns, gram = lax.optimization_barrier((exchange(columns, "dp"), gram))
    means = mean_right(membership, modality, share, columns)
    inverse, blocks = factor(share, gram, swap(gram, 1))
    own = finish(share, inverse, exchange(means, "dp"))
    own, blocks = lax.optimization_barrier((own, blocks))
    pt = orthonormal(blocks, left_mean)
    mine = [own] + [swap(own, 2 * s) for s in (1, 2, 3)]
    other = [swap(piece, 1) for piece in mine]
    return tuple(error_of(share, mine, other, pt, merged))


def solution(mesh):
    in_specs = (
        P("dp", None, None, "expert"),
        P("dp", None, None, None),
        P("dp", None, "expert", None),
        P(),
        P(),
        P(),
    )
    out_specs = (P("dp", None, None), P("dp", None, "expert", None))
    return jax.shard_map(
        on_device, mesh=mesh, in_specs=in_specs, out_specs=out_specs, check_vma=False
    )
```
